32 devices in a mesh: edge: 16 (over z, y, x), rep: 2 (over core).
Axes of the slice: x: 2, y: 2, z: 4, core: 2. Of those that a mesh axis runs over, the one named last changes fastest.
Arguments:
- edge_feats: bfloat16 [65536, 512], P(('rep', 'edge')), parts along dimension 0, may hold values from -6 to 6
- atom_feats: bfloat16 [8192, 512], P(('rep', 'edge')), parts along dimension 0, may hold values from -6 to 6
- w_edge: bfloat16 [6, 512, 512], replicated, may hold values from -0.25 to 0.25
- w_atom: bfloat16 [2, 512, 512], replicated, may hold values from -0.25 to 0.25
- send_order: int32 [32, 2048], P(('rep', 'edge')), parts along dimension 0, may hold values from 0 to 2047, as said below
- recv_pos: int32 [32, 2048], P(('rep', 'edge')), parts along dimension 0, may hold values from 0 to 2047, as said below
- edge_list: int32 [32, 2048], P(('rep', 'edge')), parts along dimension 0, may hold values from 0 to 7, never falling along the last dimension, each value on 1 to 768 neighbouring positions
- edge_atom: int32 [32, 2048], P(('rep', 'edge')), parts along dimension 0, may hold values from 0 to 127
- list_block: int32 [32, 8], P(('rep', 'edge')), parts along dimension 0, may hold values from 0 to 31, as said below
- block_home: int32 [64], P('rep'), parts along dimension 0, may hold values from 0 to 31, as said below
Outputs:
- edge_out: bfloat16 [65536, 512], P(('rep', 'edge')), parts along dimension 0
- atom_out: bfloat16 [8192, 512], P(('rep', 'edge')), parts along dimension 0
The draws below stay inside these ranges and needn't reach their ends.
There are 2 independent parts, one for each index of `rep`. The reference program is written for one: setup_inputs(seed, part) draws one part's arguments, and reference() takes and returns one part's arrays. A program takes and returns all parts, laid end to end along the dimension named above; an argument that names none is the same for every part. Nothing has to cross between parts.
Inputs may be any that keep to these rules, and one draw needn't show every extreme that they name: Each row of send_order is a permutation of the device's rows; each row of recv_pos is a permutation of the places. Every edge has exactly 128 reverse partners' messages passing between its device and each device, the pairing is symmetric, and no edge is its own partner. `recv_pos`: together with send_order the pairing of every edge with its reverse edge as described there. `list_block`: the 8 lists of one device aim at atom blocks stored on 8 different devices. `block_home`: A permutation of the block ids' storage positions.
All inputs are finite; a program needn't handle non-finite values.
Results may differ from the reference program's by a relative error of at most 0.0095.
Values may be sent and summed in bfloat16 or wider, within the bound.
No kernel may reach another device: no remote copies, remote signals or barrier semaphores. Data moves between devices by JAX's collectives and lax.ppermute only.
A program may use at most 128 MiB of HBM per device.

```python
import math
import jax
import jax.numpy as jnp
import numpy as np
from jax import lax

H = 512
ABLK = 128
BLOCKS = 2
E_DEV = 2048
AB_DEV = 2
LISTS = 8
LIST_MOST = 768
CAP = 128
NB = 32
EDGES = 32768
N_EDGE = 16


def pairing(key):
    key = jax.random.fold_in(key, 11)
    keys = jax.random.split(key, N_EDGE)
    row_order = jax.vmap(lambda k: jax.random.permutation(k, E_DEV))(keys).astype(jnp.int32)
    slots = jnp.arange(E_DEV, dtype=jnp.int32)
    group = slots // CAP
    within = slots % CAP
    devices = jnp.arange(N_EDGE, dtype=jnp.int32)[:, None]
    places = jnp.where(group[None, :] == devices, group[None, :] * CAP + CAP - 1 - within[None, :], slots[None, :])
    received = jnp.zeros((N_EDGE, E_DEV), jnp.int32).at[devices, row_order].set(places.astype(jnp.int32))
    return (row_order, received)


def placing(key):
    key = jax.random.fold_in(key, 23)
    first_key, second_key, third_key = jax.random.split(key, 3)
    home = jax.random.permutation(first_key, NB).astype(jnp.int32)
    inverse = jnp.zeros((NB,), jnp.int32).at[home].set(jnp.arange(NB, dtype=jnp.int32))
    keys = jax.random.split(second_key, N_EDGE)
    owners = jax.vmap(lambda k: jax.random.permutation(k, N_EDGE)[:LISTS])(keys).astype(jnp.int32)
    slots = jax.random.randint(third_key, (N_EDGE, LISTS), 0, AB_DEV).astype(jnp.int32)
    blocks = inverse[owners * AB_DEV + slots]
    return (blocks, home)


def draw_send_order(key, part):
    return pairing(key)[0]


def draw_recv_pos(key, part):
    return pairing(key)[1]


def draw_list_block(key, part):
    return placing(key)[0]


def draw_block_home(key, part):
    return placing(key)[1]


def plant(drawn, stream_key, least, largest):
    longest = drawn.shape.index(max(drawn.shape))
    spots = []
    for shift in (0, 1):
        where = [jax.random.randint(jax.random.fold_in(stream_key, axis), (), 0, length) for axis, length in enumerate(drawn.shape)]
        where[longest] = (where[longest] + shift) % drawn.shape[longest]
        spots.append(tuple(where))
    return drawn.at[spots[0]].set(least).at[spots[1]].set(largest)


def shard_levels(own_key, shape, shards, low, top_value):
    def one(dim, shards_of):
        heights = jax.random.uniform(jax.random.fold_in(jax.random.fold_in(own_key, 6), dim), (shards_of,), jnp.float32, low / len(shards), top_value / len(shards))
        return jnp.repeat(jnp.exp(heights), shape[dim] // shards_of).reshape((-1,) + (1,) * (len(shape) - dim - 1))

    factor_of = one(*shards[0])
    for cut in shards[1:]:
        factor_of = factor_of * one(*cut)
    return factor_of


def length_profile(count, total, bound, lean):
    loads = [(1 << 20) // math.isqrt(rank ** lean) + 1 for rank in range(2, count + 1)]
    rest, holding = total - bound - (count - 1), [1] * (count - 1)
    while rest > 0:
        candidates = [i for i in range(count - 1) if holding[i] < bound]
        mass, remaining = sum([loads[i] for i in candidates]), rest
        for i in candidates:
            addition = min(bound - holding[i], max(1, remaining * loads[i] // mass), rest)
            holding[i] = holding[i] + addition
            rest = rest - addition
    return np.array([bound] + holding)


def ragged(own_key, count, total, bound, skew):
    if count == 2:
        one = jax.random.randint(own_key, (), max(1, total - bound), min(bound, total - 1) + 1)
        return jnp.stack([one, total - one])
    tallies = jnp.asarray(length_profile(count, total, bound, skew), jnp.int32)
    couples = (count - 1) // 2
    source_of, sink = tallies[1:1 + 2 * couples:2], tallies[2:2 + 2 * couples:2]
    slack = jnp.minimum(source_of - 1, bound - sink)
    passed = jax.random.randint(jax.random.fold_in(own_key, 1), (couples,), 0, 1 << 20) % (slack + 1)
    tallies = tallies.at[1:1 + 2 * couples:2].set(source_of - passed).at[2:2 + 2 * couples:2].set(sink + passed)
    return tallies[jax.random.permutation(jax.random.fold_in(own_key, 2), count)]


def gaussian(stream_key, shape, spread, most, cuts=(), kind=jnp.bfloat16):
    drawn = jax.random.normal(stream_key, shape, jnp.float32) * spread
    if len(cuts) > 0:
        drawn = shard_levels(stream_key, shape, cuts, -0.22, 0.18) * drawn
    return jnp.clip(drawn, min=-most, max=most).astype(kind)


def setup_inputs(seed: int = 0, part: int = 0) -> dict:
    arg_keys = jax.random.split(jax.random.key(seed), 11)
    part_splits = jax.random.split(jax.random.fold_in(arg_keys[10], part), 11)
    edge_feats = gaussian(part_splits[0], (EDGES, H), 1.0, 6.0, ((0, 16),))
    atom_feats = gaussian(part_splits[1], (NB * ABLK, H), 1.0, 6.0, ((0, 16),))
    w_edge = gaussian(arg_keys[2], (3 * BLOCKS, H, H), H ** -0.5, 0.25)
    w_atom = gaussian(arg_keys[3], (BLOCKS, H, H), H ** -0.5, 0.25)
    send_order = draw_send_order(jax.random.fold_in(jax.random.fold_in(arg_keys[10], part), 71), part)
    recv_pos = draw_recv_pos(jax.random.fold_in(jax.random.fold_in(arg_keys[10], part), 71), part)
    edge_list = jax.vmap(lambda own: jnp.searchsorted(jnp.cumsum(ragged(own, LISTS, E_DEV, LIST_MOST, 2)), jnp.arange(E_DEV), side="right"))(jax.random.split(part_splits[6], N_EDGE)).reshape((N_EDGE, E_DEV)).astype(jnp.int32)
    edge_atom = plant(jax.random.randint(part_splits[7], (N_EDGE, E_DEV), 0, ABLK), jax.random.fold_in(part_splits[7], 1), 0, ABLK - 1).astype(jnp.int32)
    list_block = draw_list_block(jax.random.fold_in(jax.random.fold_in(arg_keys[10], part), 71), part)
    block_home = draw_block_home(jax.random.fold_in(jax.random.fold_in(arg_keys[10], part), 71), part)
    return {"edge_feats": edge_feats, "atom_feats": atom_feats, "w_edge": w_edge, "w_atom": w_atom, "send_order": send_order, "recv_pos": recv_pos, "edge_list": edge_list, "edge_atom": edge_atom, "list_block": list_block, "block_home": block_home}


def dense_silu(values, weight):
    return jax.nn.silu(jnp.dot(values, weight, preferred_element_type=jnp.float32)).astype(jnp.bfloat16)


def reference(edge_feats, atom_feats, w_edge, w_atom, send_order, recv_pos, edge_list, edge_atom, list_block, block_home):
    devices = jnp.arange(N_EDGE, dtype=jnp.int32)[:, None]
    source = recv_pos // CAP
    within = recv_pos % CAP
    source_row = send_order[source, devices * CAP + within]
    partner = (source * E_DEV + source_row).reshape(-1).astype(jnp.int32)
    list_pos = block_home[list_block]
    edge_pos = jnp.take_along_axis(list_pos, edge_list, axis=1)
    target = (edge_pos * ABLK + edge_atom).reshape(-1).astype(jnp.int32)
    seg_keys = (edge_list * ABLK + edge_atom).astype(jnp.int32)
    message = edge_feats
    atoms = atom_feats
    for layer_block in range(BLOCKS):
        first = dense_silu(message, w_edge[3 * layer_block])
        second = dense_silu(first, w_edge[3 * layer_block + 1])
        paired = (second.astype(jnp.float32) + second[partner].astype(jnp.float32)).astype(jnp.bfloat16)
        third = dense_silu(paired, w_edge[3 * layer_block + 2])

        def add_device(total, items):
            rows, keys, places = items
            part = jax.ops.segment_sum(rows.astype(jnp.float32), keys, num_segments=LISTS * ABLK)
            part = part.astype(jnp.bfloat16).astype(jnp.float32).reshape(LISTS, ABLK, H)
            return total.at[places].add(part), None

        start = jnp.zeros((NB, ABLK, H), jnp.float32)
        gathered, _ = lax.scan(add_device, start, (third.reshape(N_EDGE, E_DEV, H), seg_keys, list_pos))
        gathered = gathered.reshape(NB * ABLK, H).astype(jnp.bfloat16)
        update = jax.nn.silu(jnp.dot(gathered, w_atom[layer_block], preferred_element_type=jnp.float32))
        atoms = (atoms.astype(jnp.float32) + update).astype(jnp.bfloat16)
        message = (message.astype(jnp.float32) + third.astype(jnp.float32) + atoms[target].astype(jnp.float32)).astype(jnp.bfloat16)
    return message, atoms
```

```python
import functools

import jax
import jax.numpy as jnp
from jax import lax
from jax.experimental import pallas as pl
from jax.experimental.pallas import tpu as pltpu
from jax.sharding import PartitionSpec as P


BLOCKS = 2
AB_DEV = 2
CHUNKS = 2
STEP_ROWS = 512
F32 = jnp.float32
BF16 = jnp.bfloat16
VMEM = pl.BlockSpec(memory_space=pltpu.VMEM)
SMEM = pl.BlockSpec(memory_space=pltpu.SMEM)


def silu(x):
    return x / (1.0 + jnp.exp(-x))


def dot(x, y):
    return jnp.dot(x, y, preferred_element_type=F32)


def hot(rows, cols, dim, values, base=0):
    spots = lax.broadcasted_iota(jnp.int32, (rows, cols), dim) + base
    return jnp.where(spots == values, 1.0, 0.0).astype(BF16)


def whole(shape):
    return pl.BlockSpec(shape, lambda i: (0,) * len(shape))


def rows_spec(rows, cols):
    return pl.BlockSpec((rows, cols), lambda i: (i, 0))


def params():
    return pltpu.CompilerParams(vmem_limit_bytes=56 * 1024 * 1024)


def cost(flops, moved):
    return pl.CostEstimate(flops=flops, bytes_accessed=moved, transcendentals=0)


def store_blocks(step, steps, refs, value, cap):
    per = len(refs) // steps
    for i in range(steps):

        @pl.when(step == i)
        def _(i=i):
            for j in range(per):
                refs[i * per + j][...] = value[j * cap : (j + 1) * cap]


def two_dense(x, first_w, second_w):
    first = silu(dot(x, first_w[...])).astype(BF16)
    return silu(dot(first, second_w[...])).astype(BF16)


def start_kernel(steps, cap, cols, feats, w0, w1, msg, *secs):
    step = pl.program_id(0)
    picked = hot(cols.shape[0], feats.shape[0], 1, cols[:, 0:1])
    x = dot(picked, feats[...]).astype(BF16)
    msg[...] = x
    store_blocks(step, steps, secs, two_dense(x, w0, w1), cap)


def start_call(cols, feats, w0, w1, peers, step_rows):
    rows, feat = feats.shape
    cap = rows // peers
    steps = rows // step_rows
    block = jax.ShapeDtypeStruct((cap, feat), BF16)
    out = pl.pallas_call(
        functools.partial(start_kernel, steps, cap),
        grid=(steps,),
        in_specs=[
            rows_spec(step_rows, cols.shape[1]),
            whole((rows, feat)),
            whole(w0.shape),
            whole(w1.shape),
        ],
        out_specs=[rows_spec(step_rows, feat)] + [whole((cap, feat))] * peers,
        out_shape=[jax.ShapeDtypeStruct((rows, feat), BF16)] + [block] * peers,
        compiler_params=params(),
        cost_estimate=cost(2 * rows * feat * (rows + 2 * feat), 8 * rows * feat),
        name="start",
    )(cols, feats, w0, w1)
    return out[0], out[1:]


def third_kernel(peers, steps, outer, inner, chunks, cols, keys, lids, w2, *refs):
    secs, arrived = refs[:peers], refs[peers : 2 * peers]
    third = refs[2 * peers]
    sends = refs[2 * peers + 1 : 2 * peers + 1 + chunks * inner]
    sec_tmp, arr_tmp, part = refs[2 * peers + 1 + chunks * inner :]
    step = pl.program_id(0)
    step_rows = sec_tmp.shape[0]
    cap = secs[0].shape[0]
    per = peers // steps
    for i in range(steps):

        @pl.when(step == i)
        def _(i=i):
            for j in range(per):
                sec_tmp[j * cap : (j + 1) * cap] = secs[i * per + j][...]
                arr_tmp[j * cap : (j + 1) * cap] = arrived[i * per + j][...]

    pairs = []
    for j in range(per):
        span = slice(j * cap, (j + 1) * cap)
        back = dot(hot(cap, cap, 1, cols[span, 1:2]), arr_tmp[span])
        pairs.append((sec_tmp[span].astype(F32) + back).astype(BF16))
    paired = jnp.concatenate(pairs, axis=0)
    start = pl.multiple_of(step * step_rows, step_rows)
    third[pl.ds(start, step_rows), :] = silu(dot(paired, w2[...])).astype(BF16)

    @pl.when(step == steps - 1)
    def _():
        tile = min(step_rows, part.shape[0])

        def summed(m, carry):
            base = pl.multiple_of(m * tile, tile)
            match = hot(tile, third.shape[0], 0, keys[...], base)
            part[pl.ds(base, tile), :] = dot(match, third[...]).astype(BF16)
            return carry

        lax.fori_loop(0, part.shape[0] // tile, summed, 0)
        rows = sends[0].shape[1]
        for k in range(inner):
            for h in range(outer):
                lid = lids[k * outer + h]

                @pl.when(lid >= 0)
                def _(k=k, h=h, lid=lid):
                    for c in range(chunks):
                        spot = pl.multiple_of(lid * (rows * chunks) + c * rows, rows)
                        sends[c * inner + k][h] = part[pl.ds(spot, rows), :]

                @pl.when(lid < 0)
                def _(k=k, h=h):
                    for c in range(chunks):
                        zero = jnp.zeros((rows, third.shape[1]), BF16)
                        sends[c * inner + k][h] = zero


def third_call(cols, keys, lids, w2, secs, arrived, outer, inner, ablk, lists, step_rows):
    peers = len(secs)
    cap, feat = secs[0].shape
    rows = cap * peers
    steps = rows // step_rows
    piece = (outer, ablk // CHUNKS, feat)
    out = pl.pallas_call(
        functools.partial(third_kernel, peers, steps, outer, inner, CHUNKS),
        grid=(steps,),
        in_specs=[
            rows_spec(step_rows, cols.shape[1]),
            whole(keys.shape),
            SMEM,
            whole(w2.shape),
        ]
        + [whole((cap, feat))] * (2 * peers),
        out_specs=[whole((rows, feat))] + [whole(piece)] * (CHUNKS * inner),
        out_shape=[jax.ShapeDtypeStruct((rows, feat), BF16)]
        + [jax.ShapeDtypeStruct(piece, BF16)] * (CHUNKS * inner),
        scratch_shapes=[
            pltpu.VMEM((step_rows, feat), BF16),
            pltpu.VMEM((step_rows, feat), BF16),
            pltpu.VMEM((lists * ablk, feat), BF16),
        ],
        compiler_params=params(),
        cost_estimate=cost(2 * rows * feat * (lists * ablk + feat), 10 * rows * feat),
        name="third",
    )(cols, keys, lids, w2, *secs, *arrived)
    sends = [list(out[1 + c * inner : 1 + (c + 1) * inner]) for c in range(CHUNKS)]
    return out[0], sends


def plane_kernel(outer, inner, slots, rids, place, *refs):
    got, outs = refs[:inner], refs[inner:]
    for j in range(outer):
        h = place[0] ^ j
        for s in range(slots):
            total = jnp.zeros(outs[0].shape[1:], F32)
            for k in range(inner):
                mine = rids[k * outer + h] == s
                total += jnp.where(mine, got[k][h].astype(F32), 0.0)
            outs[j][s] = total.astype(BF16)


def plane_call(rids, place, got, outer, inner, slots):
    piece = (slots,) + got[0].shape[1:]
    return pl.pallas_call(
        functools.partial(plane_kernel, outer, inner, slots),
        in_specs=[SMEM, SMEM] + [VMEM] * inner,
        out_specs=[VMEM] * outer,
        out_shape=[jax.ShapeDtypeStruct(piece, BF16)] * outer,
        compiler_params=params(),
        cost_estimate=cost(0, 2 * outer * inner * piece[1] * piece[2] * 2),
        name="plane",
    )(rids, place, *got)


def update_kernel(atoms, w, *refs):
    got, out = refs[:-1], refs[-1]
    total = got[0][...].astype(F32)
    for ref in got[1:]:
        total += ref[...].astype(F32)
    slots, rows, feat = out.shape
    gathered = total.astype(BF16).reshape(slots * rows, feat)
    update = silu(dot(gathered, w[...])).reshape(slots, rows, feat)
    out[...] = (atoms[...].astype(F32) + update).astype(BF16)


def update_call(atoms, w, got):
    return pl.pallas_call(
        update_kernel,
        in_specs=[VMEM] * (2 + len(got)),
        out_specs=VMEM,
        out_shape=jax.ShapeDtypeStruct(atoms.shape, BF16),
        compiler_params=params(),
        cost_estimate=cost(2 * atoms.size * w.shape[0], 2 * w.size + 12 * atoms.size),
        name="update",
    )(atoms, w, *got)


def answer_kernel(outer, inner, rids, place, *refs):
    got, outs = refs[:outer], refs[outer:]
    for j in range(outer):
        h = place[0] ^ j
        for k in range(inner):
            slot = jnp.maximum(rids[k * outer + h], 0)
            outs[k][h] = got[j][slot]


def answer_call(rids, place, got, outer, inner):
    piece = (outer,) + got[0].shape[1:]
    return pl.pallas_call(
        functools.partial(answer_kernel, outer, inner),
        in_specs=[SMEM, SMEM] + [VMEM] * outer,
        out_specs=[VMEM] * inner,
        out_shape=[jax.ShapeDtypeStruct(piece, BF16)] * inner,
        compiler_params=params(),
        cost_estimate=cost(0, 4 * inner * piece[0] * piece[1] * piece[2]),
        name="answer",
    )(rids, place, *got)


def fill_home(spots, homes, home, outer, inner, chunks):
    rows = homes[0].shape[1]
    lists = home.shape[0] // (rows * chunks)

    def fill(l, carry):
        spot = spots[l]
        for k in range(inner):

            @pl.when(spot // outer == k)
            def _(k=k):
                for c in range(chunks):
                    base = pl.multiple_of(l * (rows * chunks) + c * rows, rows)
                    home[pl.ds(base, rows), :] = homes[c * inner + k][spot % outer]

        return carry

    lax.fori_loop(0, lists, fill, 0)


def next_kernel(steps, cap, outer, inner, chunks, spots, cols, msg, third, w0, w1, *refs):
    homes = refs[: chunks * inner]
    new_msg = refs[chunks * inner]
    secs = refs[chunks * inner + 1 : -1]
    home = refs[-1]
    step = pl.program_id(0)

    @pl.when(step == 0)
    def _():
        fill_home(spots, homes, home, outer, inner, chunks)

    fetched = dot(hot(cols.shape[0], home.shape[0], 1, cols[:, 2:3]), home[...])
    x = (msg[...].astype(F32) + third[...].astype(F32) + fetched).astype(BF16)
    new_msg[...] = x
    store_blocks(step, steps, secs, two_dense(x, w0, w1), cap)


def next_call(spots, cols, msg, third, w0, w1, homes, outer, inner, ablk, step_rows, peers):
    rows, feat = msg.shape
    cap = rows // peers
    steps = rows // step_rows
    lists = spots.shape[0]
    block = jax.ShapeDtypeStruct((cap, feat), BF16)
    out = pl.pallas_call(
        functools.partial(next_kernel, steps, cap, outer, inner, CHUNKS),
        grid=(steps,),
        in_specs=[
            SMEM,
            rows_spec(step_rows, cols.shape[1]),
            rows_spec(step_rows, feat),
            rows_spec(step_rows, feat),
            whole(w0.shape),
            whole(w1.shape),
        ]
        + [whole(homes[0].shape)] * len(homes),
        out_specs=[rows_spec(step_rows, feat)] + [whole((cap, feat))] * peers,
        out_shape=[jax.ShapeDtypeStruct((rows, feat), BF16)] + [block] * peers,
        scratch_shapes=[pltpu.VMEM((lists * ablk, feat), BF16)],
        compiler_params=params(),
        cost_estimate=cost(2 * rows * feat * (lists * ablk + 2 * feat), 12 * rows * feat),
        name="next",
    )(spots, cols, msg, third, w0, w1, *homes)
    return out[0], out[1:]


def order_kernel(order, msg, third, base):
    rows = base.shape[0]
    start = pl.program_id(0) * rows
    picked = hot(rows, msg.shape[0], 0, order[...], start)
    base[...] = dot(picked, msg[...]) + dot(picked, third[...])


def order_call(order, msg, third, step_rows):
    rows, feat = msg.shape
    return pl.pallas_call(
        order_kernel,
        grid=(rows // step_rows,),
        in_specs=[whole(order.shape), whole(msg.shape), whole(msg.shape)],
        out_specs=rows_spec(step_rows, feat),
        out_shape=jax.ShapeDtypeStruct((rows, feat), F32),
        compiler_params=params(),
        cost_estimate=cost(4 * rows * rows * feat, 8 * rows * feat),
        name="order",
    )(order, msg, third)


def last_kernel(outer, inner, chunks, spots, cols, base, *refs):
    homes, out, home = refs[: chunks * inner], refs[-2], refs[-1]

    @pl.when(pl.program_id(0) == 0)
    def _():
        fill_home(spots, homes, home, outer, inner, chunks)

    fetched = dot(hot(cols.shape[0], home.shape[0], 1, cols[:, 3:4]), home[...])
    out[...] = (base[...] + fetched).astype(BF16)


def last_call(spots, cols, base, homes, outer, inner, ablk, step_rows):
    rows, feat = base.shape
    lists = spots.shape[0]
    return pl.pallas_call(
        functools.partial(last_kernel, outer, inner, CHUNKS),
        grid=(rows // step_rows,),
        in_specs=[SMEM, rows_spec(step_rows, cols.shape[1]), rows_spec(step_rows, feat)]
        + [whole(homes[0].shape)] * len(homes),
        out_specs=rows_spec(step_rows, feat),
        out_shape=jax.ShapeDtypeStruct((rows, feat), BF16),
        scratch_shapes=[pltpu.VMEM((lists * ablk, feat), BF16)],
        compiler_params=params(),
        cost_estimate=cost(2 * rows * feat * lists * ablk, 8 * rows * feat),
        name="last",
    )(spots, cols, base, *homes)


def on_device(
    edge_feats,
    atom_feats,
    w_edge,
    w_atom,
    send_order,
    recv_pos,
    edge_list,
    edge_atom,
    list_block,
    block_home,
):
    peers = lax.axis_size("edge")
    me = lax.axis_index("edge").astype(jnp.int32)
    rows, feat = edge_feats.shape
    cap = rows // peers
    lists = list_block.shape[1]
    ablk = atom_feats.shape[0] // AB_DEV
    inner = 1 << ((peers.bit_length() - 1) // 2)
    outer = peers // inner
    step_rows = min(STEP_ROWS, rows)
    chunk_rows = ablk // CHUNKS

    def swap(value, offset):
        return lax.ppermute(value, "edge", [(i, i ^ offset) for i in range(peers)])

    table = jnp.arange(peers, dtype=jnp.int32)
    order = jnp.take(send_order[0].reshape(peers, cap), me ^ table, axis=0).reshape(rows)
    edge_key = edge_list[0] * ablk + edge_atom[0]
    packed = jnp.take((recv_pos[0] % cap) * (lists * ablk) + edge_key, order)
    within = packed // (lists * ablk)
    key = packed % (lists * ablk)
    cols = jnp.stack([order, within, key, edge_key], axis=1)
    key_row = key[None, :]
    order_row = order[None, :]

    block_table = jnp.arange(block_home.shape[0], dtype=jnp.int32)
    found = list_block[0][:, None] == block_table[None, :]
    list_place = jnp.sum(jnp.where(found, block_home[None, :], 0), axis=1)
    owner = list_place // AB_DEV
    slot = list_place % AB_DEV
    low, high = me % inner, me // inner
    spots = (low ^ (owner % inner)) * outer + owner // inner
    aims = spots[None, :] == table[:, None]
    lids = jnp.max(jnp.where(aims, jnp.arange(lists, dtype=jnp.int32)[None, :], -1), axis=1)
    sids = jnp.max(jnp.where(aims, slot[None, :], -1), axis=1).reshape(inner, outer)
    rids = jnp.concatenate([sids[:1]] + [swap(sids[k : k + 1], k) for k in range(1, inner)])
    rids = rids.reshape(peers)
    place = high.reshape(1)

    stored = atom_feats.reshape(AB_DEV, CHUNKS, chunk_rows, feat)
    atoms = [stored[:, c] for c in range(CHUNKS)]
    message, secs = start_call(cols, edge_feats, w_edge[0], w_edge[1], peers, step_rows)
    for b in range(BLOCKS):
        arrived = [None] * peers
        for k in range(peers - 1, 0, -1):
            arrived[k] = swap(secs[k], k)
        arrived[0] = secs[0]
        third, sends = third_call(
            cols,
            key_row,
            lids,
            w_edge[3 * b + 2],
            secs,
            arrived,
            outer,
            inner,
            ablk,
            lists,
            step_rows,
        )
        if b == BLOCKS - 1:
            base = order_call(order_row, message, third, step_rows)
        homes = []
        for c in range(CHUNKS):
            got = [sends[c][0]] + [swap(sends[c][k], k) for k in range(1, inner)]
            parts = plane_call(rids, place, got, outer, inner, AB_DEV)
            sums = [parts[0]] + [swap(parts[j], j * inner) for j in range(1, outer)]
            atoms[c] = update_call(atoms[c], w_atom[b], sums)
            column = [atoms[c]] + [swap(atoms[c], j * inner) for j in range(1, outer)]
            answers = answer_call(rids, place, column, outer, inner)
            homes += [answers[0]] + [swap(answers[k], k) for k in range(1, inner)]
        if b < BLOCKS - 1:
            message, secs = next_call(
                spots,
                cols,
                message,
                third,
                w_edge[3 * b + 3],
                w_edge[3 * b + 4],
                homes,
                outer,
                inner,
                ablk,
                step_rows,
                peers,
            )
        else:
            message = last_call(spots, cols, base, homes, outer, inner, ablk, step_rows)
    atom_out = jnp.stack(atoms, axis=1).reshape(AB_DEV * ablk, feat)
    return message, atom_out


def solution(mesh):
    split = P(("rep", "edge"), None)
    placed = (split, split, P(), P(), split, split, split, split, split, P("rep"))
    return jax.shard_map(
        on_device, mesh=mesh, in_specs=placed, out_specs=(split, split), check_vma=False
    )
```

```python
import functools

import jax
import jax.numpy as jnp
from jax import lax
from jax.experimental import pallas as pl
from jax.experimental.pallas import tpu as pltpu
from jax.sharding import PartitionSpec as P


BLOCKS = 2
AB_DEV = 2
CHUNKS = 2
STEP_ROWS = 512
F32 = jnp.float32
BF16 = jnp.bfloat16
VMEM = pl.BlockSpec(memory_space=pltpu.VMEM)
SMEM = pl.BlockSpec(memory_space=pltpu.SMEM)


def silu(x):
    return x / (1.0 + jnp.exp(-x))


def dot(x, y):
    return jnp.dot(x, y, preferred_element_type=F32)


def hot(rows, cols, dim, values, base=0):
    spots = lax.broadcasted_iota(jnp.int32, (rows, cols), dim) + base
    return jnp.where(spots == values, 1.0, 0.0).astype(BF16)


def whole(shape):
    return pl.BlockSpec(shape, lambda i: (0,) * len(shape))


def rows_spec(rows, cols):
    return pl.BlockSpec((rows, cols), lambda i: (i, 0))


def params(mib):
    return pltpu.CompilerParams(vmem_limit_bytes=mib * 1024 * 1024)


def cost(flops, moved):
    return pl.CostEstimate(flops=flops, bytes_accessed=moved, transcendentals=0)


def two_dense(x, first_w, second_w):
    first = silu(dot(x, first_w)).astype(BF16)
    return silu(dot(first, second_w)).astype(BF16)


def turn_orders(orders, turned, picked):
    peers = orders.shape[0]
    me = lax.axis_index("edge")
    for k in range(peers):
        picked[k : k + 1, :] = orders[pl.ds(me ^ k, 1), :]
    turned[...] = jnp.transpose(picked[...])


def column(turned, first, count):
    parts = [turned[:, k : k + 1] for k in range(first, first + count)]
    return jnp.concatenate(parts, axis=0)


def start_kernel(first, per, orders, feats, w0, w1, msg, *refs):
    secs, (turned, picked) = refs[:-2], refs[-2:]
    turn_orders(orders, turned, picked)
    cap = turned.shape[0]
    rows = per * cap
    for t in range(len(secs) // per):
        spots = column(turned, first + t * per, per)
        x = dot(hot(rows, feats.shape[0], 1, spots), feats[...]).astype(BF16)
        msg[t * rows : (t + 1) * rows] = x
        second = two_dense(x, w0[...], w1[...])
        for j in range(per):
            secs[t * per + j][...] = second[j * cap : (j + 1) * cap]


def start_call(orders, feats, w0, w1, first, count, per):
    rows, feat = feats.shape
    peers, cap = orders.shape
    half = count * cap
    block = jax.ShapeDtypeStruct((cap, feat), BF16)
    out = pl.pallas_call(
        functools.partial(start_kernel, first, per),
        in_specs=[VMEM] * 4,
        out_specs=[VMEM] * (1 + count),
        out_shape=[jax.ShapeDtypeStruct((half, feat), BF16)] + [block] * count,
        scratch_shapes=[
            pltpu.VMEM((cap, peers), jnp.int32),
            pltpu.VMEM((peers, cap), jnp.int32),
        ],
        compiler_params=params(24),
        cost_estimate=cost(2 * half * feat * (rows + 2 * feat), 6 * rows * feat),
        name="start",
    )(orders, feats, w0, w1)
    return out[0], list(out[1:])


def index_kernel(per, ablk, orders, info, cols, keys, turned, picked):
    turn_orders(orders, turned, picked)
    peers, cap = orders.shape
    rows = per * cap
    table = jnp.transpose(info[...])
    values = table.astype(BF16)
    for t in range(peers // per):
        span = slice(t * rows, (t + 1) * rows)
        spots = column(turned, t * per, per)
        moved = dot(hot(rows, info.shape[1], 1, spots), values)
        key = (moved[:, 0:1] * ablk + moved[:, 1:2]).astype(jnp.int32)
        edge_key = (table[span, 0:1] * ablk + table[span, 1:2]).astype(jnp.int32)
        within = moved[:, 2:3].astype(jnp.int32)
        lane = lax.broadcasted_iota(jnp.int32, (rows, info.shape[0]), 1)
        packed = jnp.where(lane == 0, key, jnp.where(lane == 1, within, edge_key))
        cols[span] = packed
        keys[:, span] = jnp.transpose(packed)[0 : keys.shape[0]]


def index_call(orders, info, ablk, per):
    lanes, rows = info.shape
    peers, cap = orders.shape
    return pl.pallas_call(
        functools.partial(index_kernel, per, ablk),
        in_specs=[VMEM] * 2,
        out_specs=[VMEM] * 2,
        out_shape=[
            jax.ShapeDtypeStruct((rows, lanes), jnp.int32),
            jax.ShapeDtypeStruct((8, rows), jnp.int32),
        ],
        scratch_shapes=[
            pltpu.VMEM((cap, peers), jnp.int32),
            pltpu.VMEM((peers, cap), jnp.int32),
        ],
        compiler_params=params(24),
        cost_estimate=cost(2 * rows * rows * lanes, 8 * rows * lanes),
        name="index",
    )(orders, info)


def third_kernel(per, base, outer, inner, chunks, joins, ends, cols, keys, w2, *refs):
    refs = list(refs)
    lids = refs.pop(0) if ends else None
    acc_in = refs.pop(0) if joins else None
    secs, arrived = refs[:per], refs[per : 2 * per]
    third, refs = refs[2 * per], refs[2 * per + 1 :]
    cap = secs[0].shape[0]
    pairs = []
    for j in range(per):
        span = slice(base + j * cap, base + (j + 1) * cap)
        back = dot(hot(cap, cap, 1, cols[span, 1:2]), arrived[j][...])
        pairs.append((secs[j][...].astype(F32) + back).astype(BF16))
    value = silu(dot(jnp.concatenate(pairs, axis=0), w2[...])).astype(BF16)
    third[...] = value
    lanes = slice(base, base + per * cap)
    acc = refs.pop() if ends else refs[0]
    tile = min(512, acc.shape[0])
    for m in range(0, acc.shape[0], tile):
        total = dot(hot(tile, per * cap, 0, keys[0:1, lanes], m), value)
        if joins:
            total += acc_in[m : m + tile]
        acc[m : m + tile] = total.astype(acc.dtype)
    if not ends:
        return
    sends = refs
    rows = sends[0].shape[1]
    for k in range(inner):
        for h in range(outer):
            lid = lids[k * outer + h]

            @pl.when(lid >= 0)
            def _(k=k, h=h, lid=lid):
                for c in range(chunks):
                    spot = pl.multiple_of(lid * (rows * chunks) + c * rows, rows)
                    sends[c * inner + k][h] = acc[pl.ds(spot, rows), :]

            @pl.when(lid < 0)
            def _(k=k, h=h):
                for c in range(chunks):
                    sends[c * inner + k][h] = jnp.zeros((rows, third.shape[1]), BF16)


def third_call(cols, keys, w2, secs, arrived, acc, lids, group, outer, inner, ablk, lists):
    per = len(secs)
    cap, feat = secs[0].shape
    rows = cap * per
    joins, ends = acc is not None, lids is not None
    piece = (outer, ablk // CHUNKS, feat)
    out_shape = [jax.ShapeDtypeStruct((rows, feat), BF16)]
    scratch = []
    if ends:
        out_shape += [jax.ShapeDtypeStruct(piece, BF16)] * (CHUNKS * inner)
        scratch = [pltpu.VMEM((lists * ablk, feat), BF16)]
    else:
        out_shape += [jax.ShapeDtypeStruct((lists * ablk, feat), F32)]
    args = [cols, keys, w2]
    specs = [VMEM] * 3
    if ends:
        args, specs = args + [lids], specs + [SMEM]
    aliases = {}
    if joins:
        if not ends:
            aliases = {len(args): 1}
        args, specs = args + [acc], specs + [VMEM]
    args += [*secs, *arrived]
    specs += [VMEM] * (2 * per)
    out = pl.pallas_call(
        functools.partial(
            third_kernel, per, group * rows, outer, inner, CHUNKS, joins, ends
        ),
        in_specs=specs,
        out_specs=[VMEM] * len(out_shape),
        out_shape=out_shape,
        scratch_shapes=scratch,
        input_output_aliases=aliases,
        compiler_params=params(24),
        cost_estimate=cost(2 * rows * feat * (lists * ablk + feat), 10 * rows * feat),
        name="third",
    )(*args)
    return out[0], list(out[1:])


def plane_kernel(outer, inner, slots, rids, place, *refs):
    got, outs = refs[:inner], refs[inner:]
    for j in range(outer):
        h = place[0] ^ j
        for s in range(slots):
            total = jnp.zeros(outs[0].shape[1:], F32)
            for k in range(inner):
                mine = rids[k * outer + h] == s
                total += jnp.where(mine, got[k][h].astype(F32), 0.0)
            outs[j][s] = total.astype(BF16)


def plane_call(rids, place, got, outer, inner, slots):
    piece = (slots,) + got[0].shape[1:]
    return pl.pallas_call(
        functools.partial(plane_kernel, outer, inner, slots),
        in_specs=[SMEM, SMEM] + [VMEM] * inner,
        out_specs=[VMEM] * outer,
        out_shape=[jax.ShapeDtypeStruct(piece, BF16)] * outer,
        compiler_params=params(8),
        cost_estimate=cost(0, 2 * outer * inner * piece[1] * piece[2] * 2),
        name="plane",
    )(rids, place, *got)


def update_kernel(atoms, w, *refs):
    got, out = refs[:-1], refs[-1]
    total = got[0][...].astype(F32)
    for ref in got[1:]:
        total += ref[...].astype(F32)
    slots, rows, feat = out.shape
    gathered = total.astype(BF16).reshape(slots * rows, feat)
    update = silu(dot(gathered, w[...])).reshape(slots, rows, feat)
    out[...] = (atoms[...].astype(F32) + update).astype(BF16)


def update_call(atoms, w, got):
    return pl.pallas_call(
        update_kernel,
        in_specs=[VMEM] * (2 + len(got)),
        out_specs=VMEM,
        out_shape=jax.ShapeDtypeStruct(atoms.shape, BF16),
        compiler_params=params(8),
        cost_estimate=cost(2 * atoms.size * w.shape[0], 2 * w.size + 12 * atoms.size),
        name="update",
    )(atoms, w, *got)


def answer_kernel(outer, inner, rids, place, *refs):
    got, outs = refs[:outer], refs[outer:]
    for j in range(outer):
        h = place[0] ^ j
        for k in range(inner):
            slot = jnp.maximum(rids[k * outer + h], 0)
            outs[k][h] = got[j][slot]


def answer_call(rids, place, got, outer, inner):
    piece = (outer,) + got[0].shape[1:]
    return pl.pallas_call(
        functools.partial(answer_kernel, outer, inner),
        in_specs=[SMEM, SMEM] + [VMEM] * outer,
        out_specs=[VMEM] * inner,
        out_shape=[jax.ShapeDtypeStruct(piece, BF16)] * inner,
        compiler_params=params(8),
        cost_estimate=cost(0, 4 * inner * piece[0] * piece[1] * piece[2]),
        name="answer",
    )(rids, place, *got)


def fill_home(spots, homes, home, outer, inner, chunks):
    rows = homes[0].shape[1]
    lists = home.shape[0] // (rows * chunks)

    def fill(l, carry):
        spot = spots[l]
        for k in range(inner):

            @pl.when(spot // outer == k)
            def _(k=k):
                for c in range(chunks):
                    base = pl.multiple_of(l * (rows * chunks) + c * rows, rows)
                    home[pl.ds(base, rows), :] = homes[c * inner + k][spot % outer]

        return carry

    lax.fori_loop(0, lists, fill, 0)


def next_kernel(per, base, outer, inner, chunks, fills, count, cols, msg, w0, w1, *refs):
    refs = list(refs)
    thirds = [refs.pop(0) for _ in range(count // per)]
    if fills:
        spots = refs.pop(0)
        homes = [refs.pop(0) for _ in range(chunks * inner)]
        home = refs.pop()
        fill_home(spots, homes, home, outer, inner, chunks)
    else:
        home = refs.pop(0)
    new_msg, secs = refs[0], refs[1:]
    cap = secs[0].shape[0]
    rows = per * cap
    for t in range(count // per):
        span = slice(t * rows, (t + 1) * rows)
        keys = cols[base + t * rows : base + (t + 1) * rows, 0:1]
        fetched = dot(hot(rows, home.shape[0], 1, keys), home[...])
        x = msg[span].astype(F32) + thirds[t][...].astype(F32) + fetched
        x = x.astype(BF16)
        new_msg[span] = x
        second = two_dense(x, w0[...], w1[...])
        for j in range(per):
            secs[t * per + j][...] = second[j * cap : (j + 1) * cap]


def next_call(cols, msg, w0, w1, thirds, source, first, per, outer, inner, ablk, lists, cap):
    half, feat = msg.shape
    count = half // cap
    fills = isinstance(source, tuple)
    out_shape = [jax.ShapeDtypeStruct((half, feat), BF16)]
    out_shape += [jax.ShapeDtypeStruct((cap, feat), BF16)] * count
    args = [cols, msg, w0, w1, *thirds]
    specs = [VMEM] * len(args)
    if fills:
        spots, homes = source
        args += [spots, *homes]
        specs += [SMEM] + [VMEM] * len(homes)
        out_shape += [jax.ShapeDtypeStruct((lists * ablk, feat), BF16)]
    else:
        args += [source]
        specs += [VMEM]
    out = pl.pallas_call(
        functools.partial(
            next_kernel, per, first * cap, outer, inner, CHUNKS, fills, count
        ),
        in_specs=specs,
        out_specs=[VMEM] * len(out_shape),
        out_shape=out_shape,
        compiler_params=params(24),
        cost_estimate=cost(2 * half * feat * (lists * ablk + 2 * feat), 12 * half * feat),
        name="next",
    )(*args)
    return out[0], list(out[1 : 1 + count]), out[-1]


def order_kernel(order, *refs):
    pieces, base = refs[:-1], refs[-1]
    rows = base.shape[0]
    start = pl.program_id(0) * rows
    total = jnp.zeros(base.shape, F32)
    at = 0
    for piece in pieces:
        size = piece.shape[0]
        total += dot(hot(rows, size, 0, order[:, at : at + size], start), piece[...])
        at = (at + size) % order.shape[1]
    base[...] = total


def order_call(order, halves, thirds, step_rows):
    rows, feat = order.shape[1], halves[0].shape[1]
    pieces = [*halves, *thirds]
    return pl.pallas_call(
        order_kernel,
        grid=(rows // step_rows,),
        in_specs=[VMEM] * (1 + len(pieces)),
        out_specs=rows_spec(step_rows, feat),
        out_shape=jax.ShapeDtypeStruct((rows, feat), F32),
        compiler_params=params(24),
        cost_estimate=cost(4 * rows * rows * feat, 8 * rows * feat),
        name="order",
    )(order, *pieces)


def last_kernel(outer, inner, chunks, spots, cols, base, *refs):
    homes, out, home = refs[: chunks * inner], refs[-2], refs[-1]
    rows = out.shape[0]

    @pl.when(pl.program_id(0) == 0)
    def _():
        fill_home(spots, homes, home, outer, inner, chunks)

    keys = cols[pl.ds(pl.multiple_of(pl.program_id(0) * rows, rows), rows), 2:3]
    fetched = dot(hot(rows, home.shape[0], 1, keys), home[...])
    out[...] = (base[...] + fetched).astype(BF16)


def last_call(spots, cols, base, homes, outer, inner, ablk, step_rows):
    rows, feat = base.shape
    lists = spots.shape[0]
    return pl.pallas_call(
        functools.partial(last_kernel, outer, inner, CHUNKS),
        grid=(rows // step_rows,),
        in_specs=[SMEM, VMEM, rows_spec(step_rows, feat)] + [VMEM] * len(homes),
        out_specs=rows_spec(step_rows, feat),
        out_shape=jax.ShapeDtypeStruct((rows, feat), BF16),
        scratch_shapes=[pltpu.VMEM((lists * ablk, feat), BF16)],
        compiler_params=params(24),
        cost_estimate=cost(2 * rows * feat * lists * ablk, 8 * rows * feat),
        name="last",
    )(spots, cols, base, *homes)


def on_device(
    edge_feats,
    atom_feats,
    w_edge,
    w_atom,
    send_order,
    recv_pos,
    edge_list,
    edge_atom,
    list_block,
    block_home,
):
    peers = lax.axis_size("edge")
    me = lax.axis_index("edge").astype(jnp.int32)
    rows, feat = edge_feats.shape
    cap = rows // peers
    lists = list_block.shape[1]
    ablk = atom_feats.shape[0] // AB_DEV
    inner = 1 << ((peers.bit_length() - 1) // 2)
    outer = peers // inner
    step_rows = min(STEP_ROWS, rows // 2)
    chunk_rows = ablk // CHUNKS
    per = step_rows // cap
    half = peers // 2

    def swap(value, offset):
        return lax.ppermute(value, "edge", [(i, i ^ offset) for i in range(peers)])

    table = jnp.arange(peers, dtype=jnp.int32)
    orders = send_order[0].reshape(peers, cap)
    info = jnp.stack([edge_list[0], edge_atom[0], recv_pos[0] % cap]).astype(F32)
    info = jnp.pad(info, ((0, 125), (0, 0)))

    far_msg, far_secs = start_call(orders, edge_feats, w_edge[0], w_edge[1], half, half, per)
    near_msg, near_secs = start_call(orders, edge_feats, w_edge[0], w_edge[1], 0, half, per)
    cols, keys = index_call(orders, info, ablk, per)
    order_row = jnp.take(orders, me ^ table, axis=0).reshape(1, rows)

    block_table = jnp.arange(block_home.shape[0], dtype=jnp.int32)
    found = list_block[0][:, None] == block_table[None, :]
    list_place = jnp.sum(jnp.where(found, block_home[None, :], 0), axis=1)
    owner = list_place // AB_DEV
    slot = list_place % AB_DEV
    low, high = me % inner, me // inner
    spots = (low ^ (owner % inner)) * outer + owner // inner
    aims = spots[None, :] == table[:, None]
    lids = jnp.max(jnp.where(aims, jnp.arange(lists, dtype=jnp.int32)[None, :], -1), axis=1)
    sids = jnp.max(jnp.where(aims, slot[None, :], -1), axis=1).reshape(inner, outer)
    rids = jnp.concatenate([sids[:1]] + [swap(sids[k : k + 1], k) for k in range(1, inner)])
    rids = rids.reshape(peers)
    place = high.reshape(1)

    stored = atom_feats.reshape(AB_DEV, CHUNKS, chunk_rows, feat)
    atoms = [stored[:, c] for c in range(CHUNKS)]
    for b in range(BLOCKS):
        secs = near_secs + far_secs
        arrived = [None] * peers
        for k in list(range(half, peers)) + list(range(half - 1, 0, -1)):
            arrived[k] = swap(secs[k], k)
        arrived[0] = secs[0]
        thirds, acc = [], None
        for g in range(peers // per):
            span = slice(g * per, (g + 1) * per)
            ends = lids if g == peers // per - 1 else None
            w2 = w_edge[3 * b + 2]
            third, made = third_call(
                cols, keys, w2, secs[span], arrived[span], acc, ends, g, outer, inner, ablk, lists
            )
            thirds.append(third)
            acc = made[0]
        sends = [made[c * inner : (c + 1) * inner] for c in range(CHUNKS)]
        if b == BLOCKS - 1:
            base = order_call(order_row, [near_msg, far_msg], thirds, step_rows)
            atoms[0], base = lax.optimization_barrier((atoms[0], base))
        homes = []
        for c in range(CHUNKS):
            got = [sends[c][0]] + [swap(sends[c][k], k) for k in range(1, inner)]
            parts = plane_call(rids, place, got, outer, inner, AB_DEV)
            sums = [parts[0]] + [swap(parts[j], j * inner) for j in range(1, outer)]
            atoms[c] = update_call(atoms[c], w_atom[b], sums)
            stack = [atoms[c]] + [swap(atoms[c], j * inner) for j in range(1, outer)]
            answers = answer_call(rids, place, stack, outer, inner)
            homes += [answers[0]] + [swap(answers[k], k) for k in range(1, inner)]
        if b < BLOCKS - 1:
            w0, w1 = w_edge[3 * b + 3], w_edge[3 * b + 4]
            cut = len(thirds) // 2
            sizes = (per, outer, inner, ablk, lists, cap)
            far_msg, far_secs, home = next_call(
                cols, far_msg, w0, w1, thirds[cut:], (spots, homes), half, *sizes
            )
            near_msg, near_secs, _ = next_call(
                cols, near_msg, w0, w1, thirds[:cut], home, 0, *sizes
            )
    message = last_call(spots, cols, base, homes, outer, inner, ablk, step_rows)
    atom_out = jnp.stack(atoms, axis=1).reshape(AB_DEV * ablk, feat)
    return message, atom_out


def solution(mesh):
    split = P(("rep", "edge"), None)
    placed = (split, split, P(), P(), split, split, split, split, split, P("rep"))
    return jax.shard_map(
        on_device, mesh=mesh, in_specs=placed, out_specs=(split, split), check_vma=False
    )
```
